32 devices in a mesh: gx: 8 (over z, core), gy: 4 (over y, x).
Axes of the slice: x: 2, y: 2, z: 4, core: 2. Of those that a mesh axis runs over, the one named last changes fastest.
Arguments:
- suction_potential: float32 [64, 32, 128], P('gx', 'gy'), may hold values from -3 to 0.3
- ground_warmth: float32 [64, 32, 128], P('gx', 'gy'), may hold values from -4 to 4
- ground_category: int32 [64, 32, 128], P('gx', 'gy'), may hold values from 0 to 11
- icebound_flag: int32 [64, 32, 128], P('gx', 'gy'), may hold values 0 or 1
- ground_wetted_permeability: float32 [12], replicated, may hold values from 0.02 to 0.15
- ground_falloff_exponent: float32 [12], replicated, may hold values from 0.3 to 1.5
- camera_skew_per_plane: float32 [4], replicated, may hold values from -1 to 1
- hue_gradient_steepness: float32 [3], replicated, may hold values from 4 to 16
- hue_gradient_middles: float32 [3], replicated, may hold values from 0.1 to 0.4
- camera_distance_ordering: int32 [4, 4], replicated, may hold values from 0 to 3, as said below
Outputs:
- head_out: float32 [64, 32, 128], P('gx', 'gy')
- temp_out: float32 [64, 32, 128], P('gx', 'gy')
- image: float32 [4, 4, 64, 128], P(None, None, 'gx', 'gy')
The draws below stay inside these ranges and needn't reach their ends.
Inputs may be any that keep to these rules, and one draw needn't show every extreme that they name: Each row of camera_distance_ordering names every slab 0 to 3 once.
All inputs are finite; a program needn't handle non-finite values. No bound on the sum of `icebound_flag` on one device may be relied on, other than what follows from the above.
Results may differ from the reference program's by a relative error of at most 0.0003.
Values sent between devices are 32-bit elements; how exact they have to be, the bound alone decides.
No kernel may reach another device: no remote copies, remote signals or barrier semaphores. Data moves between devices by JAX's collectives and lax.ppermute only.
A program may use at most 64 MiB of HBM per device.

```python
import math
import jax
import jax.numpy as jnp
from jax import lax

UPRIGHT_COUNT = 128
STEPS = 2
VIEWS = 4
SOILS = 12
EASTWARD_COUNT = 64
NORTHWARD_COUNT = 32
GROUPS = 4


def draw_camera_distance_ordering(key, part):
    view_keys = jax.random.split(jax.random.fold_in(key, 7301), VIEWS)

    def one_row(row_key):
        return jax.random.permutation(row_key, jnp.arange(GROUPS, dtype=jnp.int32))
    return jax.vmap(one_row)(view_keys).astype(jnp.int32)


def touch_ends(entries, rng, smallest, top_value):
    dims = entries.shape
    index_at = [jax.random.randint(jax.random.fold_in(rng, axis), (), 0, dims[axis]) for axis in range(len(dims))]
    entries = entries.at[tuple(index_at)].set(smallest)
    longest = dims.index(max(dims))
    index_at[longest] = (index_at[longest] + 1) % dims[longest]
    return entries.at[tuple(index_at)].set(top_value)


def block_levels(key, extent, cuts, smallest, high):
    factor_of, own = 1.0, jax.random.fold_in(key, 6)
    for dim, blocks in cuts:
        draws = jnp.exp(jax.random.uniform(jax.random.fold_in(own, dim), (blocks,), jnp.float32, smallest / len(cuts), high / len(cuts)))
        factor_of = factor_of * jnp.repeat(draws, extent[dim] // blocks).reshape([-1 if axis == dim else 1 for axis in range(len(extent))])
    return factor_of


def setup_inputs(seed: int = 0) -> dict:
    key_of = jax.random.split(jax.random.key(seed), 11)
    return {
        "suction_potential": jnp.clip(-3.0 + 3.3 * jax.random.uniform(key_of[0], (EASTWARD_COUNT, NORTHWARD_COUNT, UPRIGHT_COUNT), jnp.float32) ** block_levels(key_of[0], (EASTWARD_COUNT, NORTHWARD_COUNT, UPRIGHT_COUNT), ((0, 8), (1, 4)), -0.2, 0.2), -3.0, 0.3),
        "ground_warmth": jnp.clip(jax.random.uniform(key_of[1], (EASTWARD_COUNT, NORTHWARD_COUNT, UPRIGHT_COUNT), jnp.float32, -4.0, 4.0) * block_levels(key_of[1], (EASTWARD_COUNT, NORTHWARD_COUNT, UPRIGHT_COUNT), ((0, 8), (1, 4)), -0.4, 0.0), -4.0, 4.0),
        "ground_category": touch_ends(jax.random.randint(key_of[2], (EASTWARD_COUNT, NORTHWARD_COUNT, UPRIGHT_COUNT), 0, SOILS), jax.random.fold_in(key_of[2], 1), 0, SOILS - 1).astype(jnp.int32),
        "icebound_flag": touch_ends((jax.random.randint(key_of[3], (EASTWARD_COUNT, NORTHWARD_COUNT, UPRIGHT_COUNT), 0, 2) < 1).astype(jnp.int32), jax.random.fold_in(key_of[3], 1), 0, 1),
        "ground_wetted_permeability": jnp.clip(jnp.exp(jax.random.uniform(key_of[4], (SOILS,), jnp.float32, math.log(0.02), math.log(0.15))), 0.02, 0.15),
        "ground_falloff_exponent": jnp.clip(jnp.exp(jax.random.uniform(key_of[5], (SOILS,), jnp.float32, math.log(0.3), math.log(1.5))), 0.3, 1.5),
        "camera_skew_per_plane": jnp.clip(jax.random.uniform(key_of[6], (VIEWS,), jnp.float32, -1.0, 1.0), -1.0, 1.0),
        "hue_gradient_steepness": jnp.clip(jnp.exp(jax.random.uniform(key_of[7], (3,), jnp.float32, math.log(4.0), math.log(16.0))), 4.0, 16.0),
        "hue_gradient_middles": jnp.clip(jax.random.uniform(key_of[8], (3,), jnp.float32, 0.1, 0.4), 0.1, 0.4),
        "camera_distance_ordering": draw_camera_distance_ordering(jax.random.fold_in(key_of[10], 71), 0),
    }


IMPEDANCE = 4.0
DIFFUSE = 0.12


def voxel_index_map(ground_category, table):
    total = jnp.zeros(ground_category.shape, jnp.float32)
    for number in range(table.shape[0]):
        total = total + jnp.where(ground_category == number, table[number], jnp.float32(0.0))
    return total


def advance(evolving_arrays, first_row, first_col, rows_all, cols_all):
    suction_potential, temp, conduct_sat, alpha, ice = evolving_arrays
    conduct = conduct_sat * jnp.exp(alpha * jnp.minimum(suction_potential, 0.0)) * jnp.exp(-IMPEDANCE * ice * jax.nn.sigmoid(-2.0 * temp))
    global_rows = first_row + jnp.arange(suction_potential.shape[0], dtype=jnp.int32)
    global_cols = first_col + jnp.arange(suction_potential.shape[1], dtype=jnp.int32)
    open_rows = ((global_rows[:-1] >= 0) & (global_rows[1:] <= rows_all - 1))[:, None, None]
    open_cols = ((global_cols[:-1] >= 0) & (global_cols[1:] <= cols_all - 1))[None, :, None]
    flux_rows = jnp.where(open_rows, 0.5 * (conduct[1:] + conduct[:-1]) * (suction_potential[1:] - suction_potential[:-1]), 0.0)
    flux_cols = jnp.where(open_cols, 0.5 * (conduct[:, 1:] + conduct[:, :-1]) * (suction_potential[:, 1:] - suction_potential[:, :-1]), 0.0)
    flux_up = 0.5 * (conduct[..., 1:] + conduct[..., :-1]) * (suction_potential[..., 1:] - suction_potential[..., :-1] + 1.0)
    zeros_up = jnp.zeros(suction_potential.shape[:2] + (1,), suction_potential.dtype)
    change_up = jnp.concatenate([flux_up, zeros_up], 2) - jnp.concatenate([zeros_up, flux_up], 2)
    change = (flux_rows[1:, 1:-1] - flux_rows[:-1, 1:-1]) + (flux_cols[1:-1, 1:] - flux_cols[1:-1, :-1]) + change_up[1:-1, 1:-1]
    inside = ((global_rows[1:-1] >= 0) & (global_rows[1:-1] <= rows_all - 1))[:, None, None] & ((global_cols[1:-1] >= 0) & (global_cols[1:-1] <= cols_all - 1))[None, :, None]
    head_new = jnp.where(inside, suction_potential[1:-1, 1:-1] + change, 0.0)
    vertical = jnp.concatenate([temp[..., 1:], zeros_up], 2) + jnp.concatenate([zeros_up, temp[..., :-1]], 2)
    laplace = temp[2:, 1:-1] + temp[:-2, 1:-1] + temp[1:-1, 2:] + temp[1:-1, :-2] + vertical[1:-1, 1:-1] - 6.0 * temp[1:-1, 1:-1]
    temp_new = jnp.where(inside, temp[1:-1, 1:-1] + DIFFUSE * laplace, 0.0)
    return (head_new, temp_new, conduct_sat[1:-1, 1:-1], alpha[1:-1, 1:-1], ice[1:-1, 1:-1])


def moisture(suction_potential):
    return 0.05 + 0.4 * jnp.exp(0.8 * jnp.minimum(suction_potential, 0.0))


def render(theta, first_plane, planes_all, groups, tilt, gain, middle):
    depth_z = theta.shape[2]
    planes = first_plane + jnp.arange(theta.shape[1], dtype=jnp.int32)
    shift = tilt * (planes.astype(jnp.float32) - 0.5 * planes_all)
    wrapped = shift - depth_z * jnp.floor(shift / depth_z)
    base = jnp.floor(wrapped)
    frac = wrapped - base
    lower = (jnp.arange(depth_z, dtype=jnp.int32)[None, :] + base.astype(jnp.int32)[:, None]) % depth_z
    upper = (lower + 1) % depth_z
    lower_vals = jnp.take_along_axis(theta, jnp.broadcast_to(lower[None], theta.shape), axis=2)
    upper_vals = jnp.take_along_axis(theta, jnp.broadcast_to(upper[None], theta.shape), axis=2)
    sample = (1.0 - frac)[None, :, None] * lower_vals + frac[None, :, None] * upper_vals
    shape_four = (theta.shape[0], groups, theta.shape[1] // groups, depth_z)
    sample = sample.reshape(shape_four)
    optical = sample * (8.0 / planes_all)
    before = jnp.cumsum(optical, axis=2) - optical
    weight = (1.0 - jnp.exp(-optical)) * jnp.exp(-before)
    layers = [jnp.sum(jax.nn.sigmoid(gain[color] * (sample - middle[color])) * weight, axis=2) for color in range(3)]
    layers.append(jnp.sum(optical, axis=2))
    return jnp.stack(layers, 0).transpose(2, 0, 1, 3)


def composite(pieces, ranks):
    in_front = (ranks[None, :] < ranks[:, None]).astype(jnp.float32)
    depth = pieces[:, 3]
    front = jnp.einsum('ij,jxz->ixz', in_front, depth, precision=lax.Precision.HIGHEST)
    color = jnp.sum(jnp.exp(-front)[:, None] * pieces[:, :3], axis=0)
    opacity = 1.0 - jnp.exp(-jnp.sum(depth, axis=0))
    return jnp.concatenate([color, opacity[None]], 0)


def reference(suction_potential, ground_warmth, ground_category, icebound_flag, ground_wetted_permeability, ground_falloff_exponent, camera_skew_per_plane, hue_gradient_steepness, hue_gradient_middles, camera_distance_ordering):
    evolving_arrays = (suction_potential, ground_warmth, voxel_index_map(ground_category, ground_wetted_permeability), voxel_index_map(ground_category, ground_falloff_exponent), icebound_flag.astype(jnp.float32))
    for number in range(STEPS):
        padded = tuple(jnp.pad(field, ((1, 1), (1, 1), (0, 0))) for field in evolving_arrays)
        evolving_arrays = advance(padded, -1, -1, EASTWARD_COUNT, NORTHWARD_COUNT)
    theta = moisture(evolving_arrays[0])

    def one_view(item):
        tilt, ranks = item
        pieces = render(theta, 0, NORTHWARD_COUNT, GROUPS, tilt, hue_gradient_steepness, hue_gradient_middles)
        return composite(pieces, ranks)

    image = lax.map(one_view, (camera_skew_per_plane, camera_distance_ordering))
    return evolving_arrays[0], evolving_arrays[1], image
```

```python
import functools

import jax
import jax.numpy as jnp
from jax import lax
from jax.experimental import pallas as pl
from jax.experimental.pallas import tpu as pltpu
from jax.sharding import PartitionSpec as P

STEPS = 2
IMPEDANCE = 4.0
DIFFUSE = 0.12

VMEM = pl.BlockSpec(memory_space=pltpu.VMEM)
SMEM = pl.BlockSpec(memory_space=pltpu.SMEM)


def pack_kernel(head_ref, temp_ref, soil_ref, ice_ref, out_ref):
    out_ref[0] = head_ref[...]
    out_ref[1] = temp_ref[...]
    out_ref[2] = soil_ref[...].astype(jnp.float32)
    out_ref[3] = ice_ref[...].astype(jnp.float32)


def column_of(peer, count, cols):
    at = lax.rem(lax.axis_index("gy") - peer + count, count)
    return pl.multiple_of(at * cols, cols)


def edge_kernel(count, *refs):
    blocks, (inner_ref, outer_ref) = refs[:count], refs[count:]
    rows, cols = blocks[0].shape[1:3]
    odd = lax.rem(lax.axis_index("gx"), 2)
    inner = (1 - odd) * (rows - STEPS)
    outer = odd * (rows - STEPS)
    for peer, block in enumerate(blocks):
        at = pl.ds(column_of(peer, count, cols), cols)
        inner_ref[:, :, at, :] = block[:, pl.ds(inner, STEPS)]
        outer_ref[:, :, at, :] = block[:, pl.ds(outer, STEPS)]


def conductivity(head, temp, ks, alpha, ice):
    frozen = (0.5 * IMPEDANCE) * ice * (1.0 - jnp.tanh(temp))
    return 0.5 * ks * jnp.exp(alpha * jnp.minimum(head, 0.0) - frozen)


def table_row(table_ref, lane):
    row = jnp.zeros(lane.shape, jnp.float32)
    for number in range(table_ref.shape[0]):
        row = jnp.where(lane == number, table_ref[number], row)
    return row


def scalar_floor(x):
    whole = x.astype(jnp.int32)
    return whole - (whole.astype(jnp.float32) > x).astype(jnp.int32)


def main_kernel(
    count,
    rows_count,
    ks_ref,
    alpha_ref,
    tilt_ref,
    gain_ref,
    middle_ref,
    rank_ref,
    *refs,
):
    blocks = refs[:count]
    inner_ref, outer_ref, head_ref, temp_ref, image_ref, all_ref, theta_ref = refs[count:]
    rows, cols, depth = blocks[0].shape[1:]
    width = count * cols
    strip = depth // count
    views = tilt_ref.shape[0]
    gx = lax.axis_index("gx")
    gy = lax.axis_index("gy")
    odd = lax.rem(gx, 2)

    for peer, block in enumerate(blocks):
        at = pl.ds(column_of(peer, count, cols), cols)
        all_ref[:, STEPS : STEPS + rows, at, :] = block[...]
    all_ref[:, pl.ds((1 - odd) * (rows + STEPS), STEPS)] = inner_ref[...]
    all_ref[:, pl.ds(odd * (rows + STEPS), STEPS)] = outer_ref[...]

    low = (gx > 0).astype(jnp.float32)
    high = (gx < rows_count - 1).astype(jnp.float32)
    shape = (width, depth)
    lane = lax.broadcasted_iota(jnp.int32, shape, 1)
    col = lax.broadcasted_iota(jnp.int32, shape, 0)
    up_open = lane < depth - 1
    down_open = lane > 0
    next_open = col < width - 1
    last_open = col > 0
    ks_row = table_row(ks_ref, lane)
    alpha_row = table_row(alpha_ref, lane)

    def look_up(table, index):
        return jnp.take_along_axis(table, index, axis=1, mode="promise_in_bounds")

    total = rows + 2 * STEPS
    head = [all_ref[0, r] for r in range(total)]
    temp = [all_ref[1, r] for r in range(total)]
    ice = [all_ref[3, r] for r in range(total)]
    soil = [all_ref[2, r].astype(jnp.int32) for r in range(total)]
    ks = [look_up(ks_row, s) for s in soil]
    alpha = [look_up(alpha_row, s) for s in soil]
    for step in range(STEPS):
        edge = STEPS - step
        k = [conductivity(*v) for v in zip(head, temp, ks, alpha, ice)]
        size = len(head)
        across = []
        for r in range(size - 1):
            flux = (k[r] + k[r + 1]) * (head[r + 1] - head[r])
            if r == edge - 1:
                flux = flux * low
            if r == size - edge - 1:
                flux = flux * high
            across.append(flux)
        temp[edge - 1] = temp[edge - 1] * low
        temp[size - edge] = temp[size - edge] * high
        new_head, new_temp = [], []
        for r in range(1, size - 1):
            h, t, c = head[r], temp[r], k[r]
            change = across[r] - across[r - 1]
            flux = (c + pltpu.roll(c, width - 1, 0)) * (pltpu.roll(h, width - 1, 0) - h)
            flux = jnp.where(next_open, flux, 0.0)
            change = change + (flux - pltpu.roll(flux, 1, 0))
            flux = (c + pltpu.roll(c, depth - 1, 1)) * (pltpu.roll(h, depth - 1, 1) - h + 1.0)
            flux = jnp.where(up_open, flux, 0.0)
            change = change + (flux - pltpu.roll(flux, 1, 1))
            new_head.append(h + change)
            near = temp[r - 1] + temp[r + 1]
            near = near + jnp.where(next_open, pltpu.roll(t, width - 1, 0), 0.0)
            near = near + jnp.where(last_open, pltpu.roll(t, 1, 0), 0.0)
            near = near + jnp.where(up_open, pltpu.roll(t, depth - 1, 1), 0.0)
            near = near + jnp.where(down_open, pltpu.roll(t, 1, 1), 0.0)
            new_temp.append(t + DIFFUSE * (near - 6.0 * t))
        head, temp = new_head, new_temp
        ks, alpha, ice = ks[1:-1], alpha[1:-1], ice[1:-1]

    for r in range(rows):
        theta = 0.05 + 0.4 * jnp.exp(0.8 * jnp.minimum(head[r], 0.0))
        theta_ref[r * width : (r + 1) * width] = theta
        all_ref[0, r] = head[r]
        all_ref[1, r] = temp[r]
    own = pl.ds(pl.multiple_of(gy * cols, cols), cols)
    head_ref[...] = all_ref[0, :rows, own, :]
    temp_ref[...] = all_ref[1, :rows, own, :]

    lane = lax.broadcasted_iota(jnp.int32, (rows, depth), 1)
    slab_of = lane // strip
    begin = gy * strip
    clear = [jnp.ones((rows, depth), jnp.float32) for _ in range(views)]
    thick = [jnp.zeros((rows, depth), jnp.float32) for _ in range(views)]
    shade = [[jnp.zeros((rows, depth), jnp.float32)] * 3 for _ in range(views)]
    for plane in range(cols):
        layers = []
        for slab in range(count):
            y = slab * cols + plane
            value = theta_ref[pl.ds(y, rows, stride=width), :]
            layers.append((value, pltpu.roll(value, depth - 1, 1) - value))
        for view in range(views):
            sample = None
            for slab in range(count):
                y = slab * cols + plane
                shift = tilt_ref[view] * jnp.float32(y - 0.5 * width)
                turns = scalar_floor(shift * (1.0 / depth))
                wrapped = shift - depth * turns.astype(jnp.float32)
                base = scalar_floor(wrapped)
                frac = wrapped - base.astype(jnp.float32)
                value, rise = layers[slab]
                move = (slab * strip - begin - base) & (depth - 1)
                moved = pltpu.roll(value + frac * rise, move, 1)
                sample = moved if slab == 0 else jnp.where(slab_of == slab, moved, sample)
            tau = sample * (8.0 / width)
            thick[view] = thick[view] + tau
            rest = clear[view] * jnp.exp(-tau)
            weight = 0.5 * (clear[view] - rest)
            clear[view] = rest
            for c in range(3):
                glow = jnp.tanh((0.5 * gain_ref[c]) * (sample - middle_ref[c]))
                shade[view][c] = shade[view][c] + (weight + weight * glow)

    def over_slabs(x):
        size = strip
        while size < depth:
            x = x + pltpu.roll(x, size, 1)
            size *= 2
        return x

    for view in range(views):
        rank = jnp.zeros((rows, depth), jnp.int32)
        for slab in range(count):
            rank = jnp.where(slab_of == slab, rank_ref[view, slab], rank)
        front = jnp.zeros((rows, depth), jnp.float32)
        for d in range(1, count):
            nearer = pltpu.roll(rank, d * strip, 1) < rank
            front = front + jnp.where(nearer, pltpu.roll(thick[view], d * strip, 1), 0.0)
        through = jnp.exp(-front)
        for c in range(3):
            image_ref[view, c] = over_slabs(through * shade[view][c])[:, :strip]
        image_ref[view, 3] = (1.0 - jnp.exp(-over_slabs(thick[view])))[:, :strip]


def shards(head, warmth, soil, icebound, ks, alpha, tilt, gain, middle, ranks):
    rows, cols, depth = head.shape
    count = lax.axis_size("gy")
    rows_count = lax.axis_size("gx")
    width = count * cols
    views = tilt.shape[0]
    assert depth & (depth - 1) == 0 and depth % count == 0
    assert count & (count - 1) == 0 and ranks.shape[1] == count

    packed = pl.pallas_call(
        pack_kernel,
        out_shape=jax.ShapeDtypeStruct((4, rows, cols, depth), jnp.float32),
        in_specs=[VMEM] * 4,
        out_specs=VMEM,
        name="pack",
    )(head, warmth, soil, icebound)
    blocks = [packed]
    for peer in range(1, count):
        ring = [(i, (i + peer) % count) for i in range(count)]
        blocks.append(lax.ppermute(packed, "gy", ring))

    border = jax.ShapeDtypeStruct((4, STEPS, width, depth), jnp.float32)
    inner, outer = pl.pallas_call(
        functools.partial(edge_kernel, count),
        out_shape=(border, border),
        in_specs=[VMEM] * count,
        out_specs=(VMEM, VMEM),
        name="edges",
    )(*blocks)
    pairs = [(i, i + 1) for i in range(rows_count - 1)]
    pairs = [pairs[0::2], pairs[1::2]]
    pairs = [p + [(b, a) for a, b in p] for p in pairs]
    outer = lax.ppermute(outer, "gx", pairs[1])
    inner = lax.ppermute(inner, "gx", pairs[0])

    cell = jax.ShapeDtypeStruct((rows, cols, depth), jnp.float32)
    return pl.pallas_call(
        functools.partial(main_kernel, count, rows_count),
        out_shape=(
            cell,
            cell,
            jax.ShapeDtypeStruct((views, 4, rows, depth // count), jnp.float32),
        ),
        in_specs=[SMEM] * 6 + [VMEM] * (count + 2),
        out_specs=(VMEM, VMEM, VMEM),
        scratch_shapes=[
            pltpu.VMEM((4, rows + 2 * STEPS, width, depth), jnp.float32),
            pltpu.VMEM((rows * width, depth), jnp.float32),
        ],
        name="steps_and_views",
    )(ks, alpha, tilt, gain, middle, ranks, *blocks, inner, outer)


def solution(mesh):
    cells = P("gx", "gy", None)
    return jax.shard_map(
        shards,
        mesh=mesh,
        in_specs=(cells,) * 4 + (P(),) * 6,
        out_specs=(cells, cells, P(None, None, "gx", "gy")),
        check_vma=False,
    )
```

```python
import functools

import jax
import jax.numpy as jnp
from jax import lax
from jax.experimental import pallas as pl
from jax.experimental.pallas import tpu as pltpu
from jax.sharding import PartitionSpec as P

STEPS = 2
IMPEDANCE = 4.0
DIFFUSE = 0.12

MIB = 1 << 20
VMEM = pl.BlockSpec(memory_space=pltpu.VMEM)
HBM = pl.BlockSpec(memory_space=pltpu.HBM)
SMEM = pl.BlockSpec(memory_space=pltpu.SMEM)


def pack_kernel(head_ref, temp_ref, soil_ref, ice_ref, out_ref, whole_ref, sems):
    copies = [
        pltpu.make_async_copy(soil_ref, whole_ref.at[0], sems.at[0]),
        pltpu.make_async_copy(ice_ref, whole_ref.at[1], sems.at[1]),
        pltpu.make_async_copy(head_ref, out_ref.at[0], sems.at[2]),
        pltpu.make_async_copy(temp_ref, out_ref.at[1], sems.at[3]),
    ]
    for copy in copies:
        copy.start()
    for field in range(2):
        copies[field].wait()
        out_ref[2 + field] = whole_ref[field].astype(jnp.float32)
    for copy in copies[2:]:
        copy.wait()


def column_of(peer, count, cols):
    at = lax.rem(lax.axis_index("gy") - peer + count, count)
    return pl.multiple_of(at * cols, cols)


def edge_kernel(count, *refs):
    blocks, (inner_ref, outer_ref) = refs[:count], refs[count:]
    rows, cols = blocks[0].shape[1:3]
    odd = lax.rem(lax.axis_index("gx"), 2)
    inner = (1 - odd) * (rows - STEPS)
    outer = odd * (rows - STEPS)
    for peer, block in enumerate(blocks):
        at = pl.ds(column_of(peer, count, cols), cols)
        inner_ref[:, :, at, :] = block[:, pl.ds(inner, STEPS)]
        outer_ref[:, :, at, :] = block[:, pl.ds(outer, STEPS)]


def conductivity(head, temp, ks, alpha, ice):
    frozen = (0.5 * IMPEDANCE) * ice * (1.0 - jnp.tanh(temp))
    return 0.5 * ks * jnp.exp(alpha * jnp.minimum(head, 0.0) - frozen)


def table_row(table_ref, lane):
    row = jnp.zeros(lane.shape, jnp.float32)
    for number in range(table_ref.shape[0]):
        row = jnp.where(lane == number, table_ref[number], row)
    return row


def scalar_floor(x):
    whole = x.astype(jnp.int32)
    return whole - (whole.astype(jnp.float32) > x).astype(jnp.int32)


def main_kernel(
    count,
    rows_count,
    ks_ref,
    alpha_ref,
    tilt_ref,
    gain_ref,
    middle_ref,
    rank_ref,
    *refs,
):
    blocks = refs[:count]
    inner_ref, outer_ref, head_ref, temp_ref, image_ref, all_ref, theta_ref = refs[count:]
    rows, cols, depth = blocks[0].shape[1:]
    width = count * cols
    strip = depth // count
    views = tilt_ref.shape[0]
    gx = lax.axis_index("gx")
    gy = lax.axis_index("gy")
    odd = lax.rem(gx, 2)

    for peer, block in enumerate(blocks):
        at = pl.ds(column_of(peer, count, cols), cols)
        all_ref[:, STEPS : STEPS + rows, at, :] = block[...]
    all_ref[:, pl.ds((1 - odd) * (rows + STEPS), STEPS)] = inner_ref[...]
    all_ref[:, pl.ds(odd * (rows + STEPS), STEPS)] = outer_ref[...]

    low = (gx > 0).astype(jnp.float32)
    high = (gx < rows_count - 1).astype(jnp.float32)
    shape = (width, depth)
    lane = lax.broadcasted_iota(jnp.int32, shape, 1)
    col = lax.broadcasted_iota(jnp.int32, shape, 0)
    up_open = lane < depth - 1
    down_open = lane > 0
    next_open = col < width - 1
    last_open = col > 0
    ks_row = table_row(ks_ref, lane)
    alpha_row = table_row(alpha_ref, lane)

    def look_up(table, index):
        return jnp.take_along_axis(table, index, axis=1, mode="promise_in_bounds")

    total = rows + 2 * STEPS
    head = [all_ref[0, r] for r in range(total)]
    temp = [all_ref[1, r] for r in range(total)]
    ice = [all_ref[3, r] for r in range(total)]
    soil = [all_ref[2, r].astype(jnp.int32) for r in range(total)]
    ks = [look_up(ks_row, s) for s in soil]
    alpha = [look_up(alpha_row, s) for s in soil]
    for step in range(STEPS):
        edge = STEPS - step
        k = [conductivity(*v) for v in zip(head, temp, ks, alpha, ice)]
        size = len(head)
        across = []
        for r in range(size - 1):
            flux = (k[r] + k[r + 1]) * (head[r + 1] - head[r])
            if r == edge - 1:
                flux = flux * low
            if r == size - edge - 1:
                flux = flux * high
            across.append(flux)
        temp[edge - 1] = temp[edge - 1] * low
        temp[size - edge] = temp[size - edge] * high
        new_head, new_temp = [], []
        for r in range(1, size - 1):
            h, t, c = head[r], temp[r], k[r]
            change = across[r] - across[r - 1]
            flux = (c + pltpu.roll(c, width - 1, 0)) * (pltpu.roll(h, width - 1, 0) - h)
            flux = jnp.where(next_open, flux, 0.0)
            change = change + (flux - pltpu.roll(flux, 1, 0))
            flux = (c + pltpu.roll(c, depth - 1, 1)) * (pltpu.roll(h, depth - 1, 1) - h + 1.0)
            flux = jnp.where(up_open, flux, 0.0)
            change = change + (flux - pltpu.roll(flux, 1, 1))
            new_head.append(h + change)
            near = temp[r - 1] + temp[r + 1]
            near = near + jnp.where(next_open, pltpu.roll(t, width - 1, 0), 0.0)
            near = near + jnp.where(last_open, pltpu.roll(t, 1, 0), 0.0)
            near = near + jnp.where(up_open, pltpu.roll(t, depth - 1, 1), 0.0)
            near = near + jnp.where(down_open, pltpu.roll(t, 1, 1), 0.0)
            new_temp.append(t + DIFFUSE * (near - 6.0 * t))
        head, temp = new_head, new_temp
        ks, alpha, ice = ks[1:-1], alpha[1:-1], ice[1:-1]

    for r in range(rows):
        theta = 0.05 + 0.4 * jnp.exp(0.8 * jnp.minimum(head[r], 0.0))
        theta_ref[r * width : (r + 1) * width] = theta
        all_ref[0, r] = head[r]
        all_ref[1, r] = temp[r]
    own = pl.ds(pl.multiple_of(gy * cols, cols), cols)
    head_ref[...] = all_ref[0, :rows, own, :]
    temp_ref[...] = all_ref[1, :rows, own, :]

    lane = lax.broadcasted_iota(jnp.int32, (rows, depth), 1)
    slab_of = lane // strip
    begin = gy * strip
    clear = [jnp.ones((rows, depth), jnp.float32) for _ in range(views)]
    thick = [jnp.zeros((rows, depth), jnp.float32) for _ in range(views)]
    shade = [[jnp.zeros((rows, depth), jnp.float32)] * 3 for _ in range(views)]
    for plane in range(cols):
        layers = []
        for slab in range(count):
            y = slab * cols + plane
            value = theta_ref[pl.ds(y, rows, stride=width), :]
            layers.append((value, pltpu.roll(value, depth - 1, 1) - value))
        for view in range(views):
            sample = None
            for slab in range(count):
                y = slab * cols + plane
                shift = tilt_ref[view] * jnp.float32(y - 0.5 * width)
                turns = scalar_floor(shift * (1.0 / depth))
                wrapped = shift - depth * turns.astype(jnp.float32)
                base = scalar_floor(wrapped)
                frac = wrapped - base.astype(jnp.float32)
                value, rise = layers[slab]
                move = (slab * strip - begin - base) & (depth - 1)
                moved = pltpu.roll(value + frac * rise, move, 1)
                sample = moved if slab == 0 else jnp.where(slab_of == slab, moved, sample)
            tau = sample * (8.0 / width)
            thick[view] = thick[view] + tau
            rest = clear[view] * jnp.exp(-tau)
            weight = 0.5 * (clear[view] - rest)
            clear[view] = rest
            for c in range(3):
                glow = jnp.tanh((0.5 * gain_ref[c]) * (sample - middle_ref[c]))
                shade[view][c] = shade[view][c] + (weight + weight * glow)

    def over_slabs(x):
        size = strip
        while size < depth:
            x = x + pltpu.roll(x, size, 1)
            size *= 2
        return x

    for view in range(views):
        rank = jnp.zeros((rows, depth), jnp.int32)
        for slab in range(count):
            rank = jnp.where(slab_of == slab, rank_ref[view, slab], rank)
        front = jnp.zeros((rows, depth), jnp.float32)
        for d in range(1, count):
            nearer = pltpu.roll(rank, d * strip, 1) < rank
            front = front + jnp.where(nearer, pltpu.roll(thick[view], d * strip, 1), 0.0)
        through = jnp.exp(-front)
        for c in range(3):
            image_ref[view, c] = over_slabs(through * shade[view][c])[:, :strip]
        image_ref[view, 3] = (1.0 - jnp.exp(-over_slabs(thick[view])))[:, :strip]


def shards(head, warmth, soil, icebound, ks, alpha, tilt, gain, middle, ranks):
    rows, cols, depth = head.shape
    count = lax.axis_size("gy")
    rows_count = lax.axis_size("gx")
    width = count * cols
    views = tilt.shape[0]
    assert depth & (depth - 1) == 0 and depth % count == 0
    assert count & (count - 1) == 0 and ranks.shape[1] == count

    packed = pl.pallas_call(
        pack_kernel,
        out_shape=jax.ShapeDtypeStruct((4, rows, cols, depth), jnp.float32),
        in_specs=[HBM] * 4,
        out_specs=VMEM,
        scratch_shapes=[
            pltpu.VMEM((2, rows, cols, depth), jnp.int32),
            pltpu.SemaphoreType.DMA((4,)),
        ],
        compiler_params=pltpu.CompilerParams(vmem_limit_bytes=8 * MIB),
        name="pack",
    )(*(pltpu.with_memory_space_constraint(x, pltpu.HBM) for x in (head, warmth, soil, icebound)))
    blocks = [packed]
    for peer in range(1, count):
        ring = [(i, (i + peer) % count) for i in range(count)]
        blocks.append(lax.ppermute(packed, "gy", ring))

    border = jax.ShapeDtypeStruct((4, STEPS, width, depth), jnp.float32)
    inner, outer = pl.pallas_call(
        functools.partial(edge_kernel, count),
        out_shape=(border, border),
        in_specs=[VMEM] * count,
        out_specs=(VMEM, VMEM),
        compiler_params=pltpu.CompilerParams(vmem_limit_bytes=8 * MIB),
        name="edges",
    )(*blocks)
    pairs = [(i, i + 1) for i in range(rows_count - 1)]
    pairs = [pairs[0::2], pairs[1::2]]
    pairs = [p + [(b, a) for a, b in p] for p in pairs]
    inner = lax.ppermute(inner, "gx", pairs[0])
    outer = lax.ppermute(outer, "gx", pairs[1])

    cell = jax.ShapeDtypeStruct((rows, cols, depth), jnp.float32)
    return pl.pallas_call(
        functools.partial(main_kernel, count, rows_count),
        out_shape=(
            cell,
            cell,
            jax.ShapeDtypeStruct((views, 4, rows, depth // count), jnp.float32),
        ),
        in_specs=[SMEM] * 6 + [VMEM] * (count + 2),
        out_specs=(VMEM, VMEM, VMEM),
        scratch_shapes=[
            pltpu.VMEM((4, rows + 2 * STEPS, width, depth), jnp.float32),
            pltpu.VMEM((rows * width, depth), jnp.float32),
        ],
        compiler_params=pltpu.CompilerParams(vmem_limit_bytes=24 * MIB),
        name="steps_and_views",
    )(ks, alpha, tilt, gain, middle, ranks, *blocks, inner, outer)


def solution(mesh):
    cells = P("gx", "gy", None)
    return jax.shard_map(
        shards,
        mesh=mesh,
        in_specs=(cells,) * 4 + (P(),) * 6,
        out_specs=(cells, cells, P(None, None, "gx", "gy")),
        check_vma=False,
    )
```

```python
import functools

import jax
import jax.numpy as jnp
from jax import lax
from jax.experimental import pallas as pl
from jax.experimental.pallas import tpu as pltpu
from jax.sharding import PartitionSpec as P

STEPS = 2
IMPEDANCE = 4.0
DIFFUSE = 0.12
SUB = 8

MIB = 1 << 20
VMEM = pl.BlockSpec(memory_space=pltpu.VMEM)
HBM = pl.BlockSpec(memory_space=pltpu.HBM)
SMEM = pl.BlockSpec(memory_space=pltpu.SMEM)


def f32(*shape):
    return jax.ShapeDtypeStruct(shape, jnp.float32)


def params(mib):
    return pltpu.CompilerParams(vmem_limit_bytes=mib * MIB)


def halves_fit(count, rows, cols, depth):
    width, strip, half = count * cols, depth // count, cols // 2
    if count < 3 or cols != SUB or rows % SUB or width % 2 or SUB % STEPS:
        return False

    def seen(y):
        return strip + 2 * (abs(y - width // 2) + STEPS)

    starts = [q * cols + plane for q in range(count) for plane in range(half)]
    return all(seen(y) + seen(y + half) <= depth for y in starts)


def pack_kernel(count, packed, head_ref, temp_ref, soil_ref, ice_ref, own_ref, *refs):
    sent_refs, (whole_ref, sems) = refs[:-2], refs[-2:]
    rows, cols, depth = own_ref.shape[1:]
    copies = [
        pltpu.make_async_copy(soil_ref, whole_ref.at[0], sems.at[0]),
        pltpu.make_async_copy(ice_ref, whole_ref.at[1], sems.at[1]),
        pltpu.make_async_copy(head_ref, own_ref.at[0], sems.at[2]),
        pltpu.make_async_copy(temp_ref, own_ref.at[1], sems.at[3]),
    ]
    for copy in copies:
        copy.start()
    if packed:
        gy = lax.axis_index("gy")
        strip, half = depth // count, cols // 2
        sub = lax.broadcasted_iota(jnp.int32, (SUB, depth), 0)
        lane = lax.broadcasted_iota(jnp.int32, (SUB, depth), 1)
        reach = jnp.abs(gy * cols + lax.rem(sub, half) - count * cols // 2) + STEPS
        upper = sub < half
        seen = []
        for peer in range(1, count):
            begin = lax.rem(gy + peer, count) * strip - reach
            seen.append(((lane - begin) & (depth - 1)) < strip + 2 * reach)
    for field in (2, 3, 0, 1):
        copies[field - 2 if field > 1 else field + 2].wait()
        if field > 1:
            own_ref[field] = whole_ref[field - 2].astype(jnp.float32)
        if not packed:
            continue
        for row in range(0, rows, 2):
            a, b = own_ref[field, row], own_ref[field, row + 1]
            first = jnp.where(upper, a, pltpu.roll(b, half, 0))
            second = jnp.where(upper, pltpu.roll(a, half, 0), b)
            second = pltpu.roll(second, depth // 2, 1)
            for peer in range(1, count):
                at = pl.ds(row * half, SUB)
                sent_refs[peer - 1][field, at, :] = jnp.where(seen[peer - 1], first, second)
        for row in range(rows):
            at = pl.ds(rows * half + row * STEPS, STEPS)
            sent_refs[0][field, at, :] = own_ref[field, row, cols - STEPS :, :]
            sent_refs[count - 2][field, at, :] = own_ref[field, row, :STEPS, :]


def read_row(count, packed, rows, block, peer, field, row):
    if not packed or peer == 0:
        return block[field, row]
    depth = block.shape[-1]
    half = SUB // 2
    sub = lax.broadcasted_iota(jnp.int32, (SUB, depth), 0)
    near = block[field, row // 2 * SUB : row // 2 * SUB + SUB]
    far = pltpu.roll(near, depth // 2, 1)
    if row % 2:
        near = pltpu.roll(near, half, 0)
    else:
        far = pltpu.roll(far, half, 0)
    value = jnp.where(sub < half, near, far)
    if peer in (1, count - 1):
        each = SUB // STEPS
        begin = rows * half + row // each * SUB
        border = block[field, begin : begin + SUB]
        place = SUB - STEPS if peer == 1 else 0
        move = (place - row % each * STEPS) % SUB
        border = pltpu.roll(border, move, 0) if move else border
        keep = sub >= SUB - STEPS if peer == 1 else sub < STEPS
        value = jnp.where(keep, border, value)
    return value


def columns_of(peer, count, cols):
    at = lax.rem(lax.axis_index("gy") - peer + count, count)
    return pl.ds(pl.multiple_of(at * cols, cols), cols)


def edge_kernel(count, packed, *refs):
    blocks, (inner_ref, outer_ref) = refs[:count], refs[count:]
    rows, cols = blocks[0].shape[1:3]
    odd = lax.rem(lax.axis_index("gx"), 2) == 1
    for peer, block in enumerate(blocks):
        at = columns_of(peer, count, cols)
        for field in range(4):
            for row in range(STEPS):
                low = read_row(count, packed, rows, block, peer, field, row)
                high = read_row(count, packed, rows, block, peer, field, rows - STEPS + row)
                inner_ref[field, row, at, :] = jnp.where(odd, low, high)
                outer_ref[field, row, at, :] = jnp.where(odd, high, low)


def conductivity(head, temp, ks, alpha, ice):
    frozen = (0.5 * IMPEDANCE) * ice * (1.0 - jnp.tanh(temp))
    return 0.5 * ks * jnp.exp(alpha * jnp.minimum(head, 0.0) - frozen)


class Plane:
    def __init__(self, width, depth, ks_ref, alpha_ref):
        self.width, self.depth = width, depth
        lane = lax.broadcasted_iota(jnp.int32, (width, depth), 1)
        col = lax.broadcasted_iota(jnp.int32, (width, depth), 0)
        self.up_open, self.down_open = lane < depth - 1, lane > 0
        self.next_open, self.last_open = col < width - 1, col > 0
        self.tables = []
        for table_ref in (ks_ref, alpha_ref):
            table = jnp.zeros((width, depth), jnp.float32)
            for number in range(table_ref.shape[0]):
                table = jnp.where(lane == number, table_ref[number], table)
            self.tables.append(table)

    def soil(self, index):
        index = index.astype(jnp.int32)
        return [
            jnp.take_along_axis(t, index, axis=1, mode="promise_in_bounds") for t in self.tables
        ]

    def within(self, head, k):
        flux = (k + pltpu.roll(k, self.width - 1, 0)) * (
            pltpu.roll(head, self.width - 1, 0) - head
        )
        flux = jnp.where(self.next_open, flux, 0.0)
        change = flux - pltpu.roll(flux, 1, 0)
        flux = (k + pltpu.roll(k, self.depth - 1, 1)) * (
            pltpu.roll(head, self.depth - 1, 1) - head + 1.0
        )
        flux = jnp.where(self.up_open, flux, 0.0)
        return change + (flux - pltpu.roll(flux, 1, 1))

    def near(self, t):
        total = jnp.where(self.next_open, pltpu.roll(t, self.width - 1, 0), 0.0)
        total = total + jnp.where(self.last_open, pltpu.roll(t, 1, 0), 0.0)
        total = total + jnp.where(self.up_open, pltpu.roll(t, self.depth - 1, 1), 0.0)
        return total + jnp.where(self.down_open, pltpu.roll(t, 1, 1), 0.0)


def across(k_a, head_a, k_b, head_b):
    return (k_a + k_b) * (head_b - head_a)


def middle_kernel(count, packed, ks_ref, alpha_ref, *refs):
    blocks, (head_ref, temp_ref, rim_ref, all_ref) = refs[:count], refs[count:]
    rows, cols, depth = blocks[0].shape[1:]
    plane = Plane(count * cols, depth, ks_ref, alpha_ref)
    for peer, block in enumerate(blocks):
        at = columns_of(peer, count, cols)
        for field in range(4):
            for row in range(rows):
                all_ref[field, row, at, :] = read_row(
                    count, packed, rows, block, peer, field, row
                )
    last = rows - 1
    head, temp, k, soil = [], [], [], []
    for row in range(rows):
        head.append(all_ref[0, row])
        temp.append(all_ref[1, row])
        soil.append((*plane.soil(all_ref[2, row]), all_ref[3, row]))
        k.append(conductivity(head[row], temp[row], *soil[row]))
    for side, row in ((0, 0), (1, last)):
        for number, value in enumerate((head[row], temp[row], k[row], *soil[row])):
            rim_ref[side, number] = value
    for step in range(STEPS):
        first, end = step, last - step
        fluxes = {
            row: across(k[row], head[row], k[row + 1], head[row + 1]) for row in range(first, end)
        }
        new_head, new_temp = {}, {}
        for row in range(first, end + 1):
            change, near = plane.within(head[row], k[row]), plane.near(temp[row])
            if row < end:
                change, near = change + fluxes[row], near + temp[row + 1]
            if row > first:
                change, near = change - fluxes[row - 1], near + temp[row - 1]
            new_head[row] = head[row] + change
            new_temp[row] = temp[row] + DIFFUSE * (near - 6.0 * temp[row])
        final = range(first, end + 1) if step == STEPS - 1 else (first, end)
        for row in final:
            head_ref[row] = new_head[row]
            temp_ref[row] = new_temp[row]
        if step == STEPS - 1:
            break
        head, temp = new_head, new_temp
        k = {r: conductivity(head[r], temp[r], *soil[r]) for r in range(first + 1, end)}
        for side, row in ((0, first + 1), (1, end - 1)):
            for number, value in enumerate((head[row], temp[row], k[row])):
                rim_ref[side, 6 + number] = value


def scalar_floor(x):
    whole = x.astype(jnp.int32)
    return whole - (whole.astype(jnp.float32) > x).astype(jnp.int32)


def last_kernel(
    count,
    rows_count,
    cols,
    ks_ref,
    alpha_ref,
    tilt_from,
    gain_from,
    middle_from,
    rank_from,
    inner_ref,
    outer_ref,
    base_head_ref,
    base_temp_ref,
    rim_ref,
    head_out_ref,
    temp_out_ref,
    image_ref,
    head_ref,
    temp_ref,
    theta_ref,
    tilt_ref,
    gain_ref,
    middle_ref,
    rank_ref,
    sems,
):
    rows, width, depth = base_head_ref.shape
    strip = depth // count
    views = tilt_ref.shape[0]
    scalars = [
        pltpu.make_async_copy(tilt_from, tilt_ref, sems.at[2]),
        pltpu.make_async_copy(gain_from, gain_ref, sems.at[3]),
        pltpu.make_async_copy(middle_from, middle_ref, sems.at[4]),
        pltpu.make_async_copy(rank_from, rank_ref, sems.at[5]),
    ]
    for copy in scalars:
        copy.start()
    gx = lax.axis_index("gx")
    gy = lax.axis_index("gy")
    odd = lax.rem(gx, 2)
    plane = Plane(width, depth, ks_ref, alpha_ref)

    for row in range(STEPS, rows - STEPS):
        head_ref[row] = base_head_ref[row]
        temp_ref[row] = base_temp_ref[row]
    for halo_ref, side in ((inner_ref, 1 - odd), (outer_ref, odd)):
        there = jnp.where(side == 0, gx > 0, gx < rows_count - 1).astype(jnp.float32)
        near, far = 1 - side, side
        head_n, temp_n, soil_n, ice_n = [halo_ref[field, near] for field in range(4)]
        head_f, temp_f, soil_f, ice_f = [halo_ref[field, far] for field in range(4)]
        soil_n = (*plane.soil(soil_n), ice_n)
        soil_f = (*plane.soil(soil_f), ice_f)
        k_n = conductivity(head_n, temp_n, *soil_n)
        k_f = conductivity(head_f, temp_f, *soil_f)
        head_e, temp_e, k_e = [rim_ref[side, number] for number in range(3)]
        soil_e = [rim_ref[side, number] for number in range(3, 6)]
        head_i, temp_i, k_i = [rim_ref[side, number] for number in range(6, 9)]
        row_e = side * (rows - 1)
        row_i = 1 + side * (rows - 3)

        flux = across(k_n, head_n, k_e, head_e)
        change = flux + across(k_n, head_n, k_f, head_f) + plane.within(head_n, k_n)
        total = temp_e + temp_f + plane.near(temp_n)
        temp_1 = there * (temp_n + DIFFUSE * (total - 6.0 * temp_n))
        head_1 = head_n + change
        k_1 = conductivity(head_1, temp_1, *soil_n)
        head_e = base_head_ref[row_e] - there * flux
        temp_e = base_temp_ref[row_e] + DIFFUSE * (there * temp_n)
        k_e = conductivity(head_e, temp_e, *soil_e)
        flux = across(k_e, head_e, k_i, head_i)
        change = flux + there * across(k_e, head_e, k_1, head_1) + plane.within(head_e, k_e)
        total = temp_1 + temp_i + plane.near(temp_e)
        head_ref[row_e] = head_e + change
        temp_ref[row_e] = temp_e + DIFFUSE * (total - 6.0 * temp_e)
        head_ref[row_i] = base_head_ref[row_i] - flux
        temp_ref[row_i] = base_temp_ref[row_i] + DIFFUSE * temp_e

    own = pl.ds(pl.multiple_of(gy * cols, cols), cols)
    copies = [
        pltpu.make_async_copy(head_ref.at[:, own, :], head_out_ref, sems.at[0]),
        pltpu.make_async_copy(temp_ref.at[:, own, :], temp_out_ref, sems.at[1]),
    ]
    for copy in copies:
        copy.start()
    for row in range(rows):
        theta = 0.05 + 0.4 * jnp.exp(0.8 * jnp.minimum(head_ref[row], 0.0))
        theta_ref[row * width : (row + 1) * width] = theta
    for copy in scalars:
        copy.wait()

    lane = lax.broadcasted_iota(jnp.int32, (rows, depth), 1)
    slab_of = lane // strip
    begin = gy * strip
    clear = [jnp.ones((rows, depth), jnp.float32) for _ in range(views)]
    thick = [jnp.zeros((rows, depth), jnp.float32) for _ in range(views)]
    shade = [[jnp.zeros((rows, depth), jnp.float32)] * 3 for _ in range(views)]
    for place in range(cols):
        layers = []
        for slab in range(count):
            y = slab * cols + place
            value = theta_ref[pl.ds(y, rows, stride=width), :]
            layers.append((value, pltpu.roll(value, depth - 1, 1) - value))
        for view in range(views):
            sample = None
            for slab in range(count):
                y = slab * cols + place
                shift = tilt_ref[view] * jnp.float32(y - 0.5 * width)
                turns = scalar_floor(shift * (1.0 / depth))
                wrapped = shift - depth * turns.astype(jnp.float32)
                base = scalar_floor(wrapped)
                frac = wrapped - base.astype(jnp.float32)
                value, rise = layers[slab]
                move = (slab * strip - begin - base) & (depth - 1)
                moved = pltpu.roll(value + frac * rise, move, 1)
                sample = moved if slab == 0 else jnp.where(slab_of == slab, moved, sample)
            tau = sample * (8.0 / width)
            thick[view] = thick[view] + tau
            rest = clear[view] * jnp.exp(-tau)
            weight = 0.5 * (clear[view] - rest)
            clear[view] = rest
            for c in range(3):
                glow = jnp.tanh((0.5 * gain_ref[c]) * (sample - middle_ref[c]))
                shade[view][c] = shade[view][c] + (weight + weight * glow)

    def over_slabs(x):
        size = strip
        while size < depth:
            x = x + pltpu.roll(x, size, 1)
            size *= 2
        return x

    for view in range(views):
        rank = jnp.zeros((rows, depth), jnp.int32)
        for slab in range(count):
            rank = jnp.where(slab_of == slab, rank_ref[view, slab], rank)
        front = jnp.zeros((rows, depth), jnp.float32)
        for d in range(1, count):
            nearer = pltpu.roll(rank, d * strip, 1) < rank
            front = front + jnp.where(nearer, pltpu.roll(thick[view], d * strip, 1), 0.0)
        through = jnp.exp(-front)
        for c in range(3):
            image_ref[view, c] = over_slabs(through * shade[view][c])[:, :strip]
        image_ref[view, 3] = (1.0 - jnp.exp(-over_slabs(thick[view])))[:, :strip]
    for copy in copies:
        copy.wait()


def shards(head, warmth, soil, icebound, ks, alpha, tilt, gain, middle, ranks):
    rows, cols, depth = head.shape
    count = lax.axis_size("gy")
    rows_count = lax.axis_size("gx")
    width = count * cols
    views = tilt.shape[0]
    assert depth & (depth - 1) == 0 and depth % count == 0
    assert count & (count - 1) == 0 and ranks.shape[1] == count
    packed = halves_fit(count, rows, cols, depth)

    sent = []
    if packed:
        for peer in range(1, count):
            more = STEPS if peer in (1, count - 1) else 0
            sent.append(f32(4, rows * (cols // 2 + more), depth))
    fields = [
        pltpu.with_memory_space_constraint(x, pltpu.HBM) for x in (head, warmth, soil, icebound)
    ]
    own, *sent = pl.pallas_call(
        functools.partial(pack_kernel, count, packed),
        out_shape=(f32(4, rows, cols, depth), *sent),
        in_specs=[HBM] * 4,
        out_specs=(VMEM,) * (1 + len(sent)),
        scratch_shapes=[
            pltpu.VMEM((2, rows, cols, depth), jnp.int32),
            pltpu.SemaphoreType.DMA((4,)),
        ],
        compiler_params=params(8),
        name="pack",
    )(*fields)
    blocks = [own]
    for peer in range(1, count):
        ring = [(i, (i + peer) % count) for i in range(count)]
        blocks.append(lax.ppermute(sent[peer - 1] if packed else own, "gy", ring))

    border = f32(4, STEPS, width, depth)
    inner, outer = pl.pallas_call(
        functools.partial(edge_kernel, count, packed),
        out_shape=(border, border),
        in_specs=[VMEM] * count,
        out_specs=(VMEM, VMEM),
        compiler_params=params(8),
        name="edges",
    )(*blocks)
    pairs = [(i, i + 1) for i in range(rows_count - 1)]
    pairs = [pairs[0::2], pairs[1::2]]
    pairs = [p + [(b, a) for a, b in p] for p in pairs]
    outer = lax.ppermute(outer, "gx", pairs[1])
    inner = lax.ppermute(inner, "gx", pairs[0])

    all_cells = f32(rows, width, depth)
    base_head, base_temp, rim = pl.pallas_call(
        functools.partial(middle_kernel, count, packed),
        out_shape=(all_cells, all_cells, f32(2, 9, width, depth)),
        in_specs=[SMEM] * 2 + [VMEM] * count,
        out_specs=(VMEM,) * 3,
        scratch_shapes=[pltpu.VMEM((4, rows, width, depth), jnp.float32)],
        compiler_params=params(16),
        name="within",
    )(ks, alpha, *blocks)

    cell = f32(rows, cols, depth)
    scalars = [
        pltpu.with_memory_space_constraint(x, pltpu.HBM) for x in (tilt, gain, middle, ranks)
    ]
    return pl.pallas_call(
        functools.partial(last_kernel, count, rows_count, cols),
        out_shape=(cell, cell, f32(views, 4, rows, depth // count)),
        in_specs=[SMEM] * 2 + [HBM] * 4 + [VMEM] * 5,
        out_specs=(HBM, HBM, VMEM),
        scratch_shapes=[
            pltpu.VMEM((rows, width, depth), jnp.float32),
            pltpu.VMEM((rows, width, depth), jnp.float32),
            pltpu.VMEM((rows * width, depth), jnp.float32),
            *(pltpu.SMEM(x.shape, x.dtype) for x in (tilt, gain, middle, ranks)),
            pltpu.SemaphoreType.DMA((6,)),
        ],
        compiler_params=params(16),
        name="views",
    )(ks, alpha, *scalars, inner, outer, base_head, base_temp, rim)


def solution(mesh):
    cells = P("gx", "gy", None)
    return jax.shard_map(
        shards,
        mesh=mesh,
        in_specs=(cells,) * 4 + (P(),) * 6,
        out_specs=(cells, cells, P(None, None, "gx", "gy")),
        check_vma=False,
    )
```
